32 devices in a mesh: ep: 16 (over z, y, core), dp: 2 (over x).
Axes of the slice: x: 2, y: 2, z: 4, core: 2. Of those that a mesh axis runs over, the one named last changes fastest.
Arguments:
- tokens_q: bfloat16 [2048, 3584], P(('dp', 'ep')), parts along dimension 0, may hold values from -448 to 448
- token_scale: float32 [2048, 28], P(('dp', 'ep')), parts along dimension 0, may hold values from 0.003 to 0.03
- residual: bfloat16 [2048, 3584], P(('dp', 'ep')), parts along dimension 0, may hold values from -6 to 6
- expert_ids: int32 [2048, 8], P(('dp', 'ep')), parts along dimension 0, may hold values from 0 to 15, all different within a row; in each aligned block of 64 rows (0 to 63, 64 to 127, ...) at most 64 rows name the same one
- gate_values: float32 [2048, 8], P(('dp', 'ep')), parts along dimension 0, may hold values from 0.1 to 1
- w_gate: bfloat16 [16, 3584, 1024], P('ep'), may hold values from -0.09375 to 0.09375
- w_up: bfloat16 [16, 3584, 1024], P('ep'), may hold values from -0.09375 to 0.09375
- w_down: bfloat16 [16, 1024, 3584], P('ep'), may hold values from -0.1875 to 0.1875
- norm_gain: float32 [3584], replicated, may hold values from 0.5 to 1.5
Outputs:
- new_residual: bfloat16 [2048, 3584], P(('dp', 'ep')), parts along dimension 0
- next_q: bfloat16 [2048, 3584], P(('dp', 'ep')), parts along dimension 0
- next_scale: float32 [2048, 28], P(('dp', 'ep')), parts along dimension 0
The draws below stay inside these ranges and needn't reach their ends.
There are 2 independent parts, one for each index of `dp`. The reference program is written for one: setup_inputs(seed, part) draws one part's arguments, and reference() takes and returns one part's arrays. A program takes and returns all parts, laid end to end along the dimension named above; an argument that names none is the same for every part. Nothing has to cross between parts.
Inputs may be any that keep to these rules, and one draw needn't show every extreme that they name: `expert_ids`: each row names 8 different experts; among the rows of one device no expert is named by more than 64 rows, and in some devices one expert is named by exactly 64.
All inputs are finite; a program needn't handle non-finite values.
Results may differ from the reference program's by a relative error of at most 0.015.
Values may be sent and summed in bfloat16 or wider, within the bound.
No kernel may reach another device: no remote copies, remote signals or barrier semaphores. Data moves between devices by JAX's collectives and lax.ppermute only.
A program may use at most 192 MiB of HBM per device.

```python
import math
import jax
import jax.numpy as jnp
import numpy as np
from jax import lax

D = 3584
FF = 1024
QB = 128
TOP = 8
TOK_DEV = 64
EXPERTS = 16
TOKENS = 1024
CAP = 64
N_EP = 16


def steps_of(stream_key, extent, split, smallest, largest):
    def one(dim, shards_of):
        draws = jax.random.uniform(jax.random.fold_in(jax.random.fold_in(stream_key, 6), dim), (shards_of,), jnp.float32, smallest / len(split), largest / len(split))
        return jnp.repeat(jnp.exp(draws), extent[dim] // shards_of).reshape((-1,) + (1,) * (len(extent) - dim - 1))

    gain = one(*split[0])
    for cut in split[1:]:
        gain = gain * one(*cut)
    return gain


def deal_out(rng, own, number, rows, amount, top, bound, skew):
    ranking = jax.random.permutation(rng, amount)
    packed, ordinary = shares(amount, rows * top, bound, skew, True), shares(amount, rows * top, bound, skew, False)
    places = jnp.arange(amount)

    def named(lengths, turn):
        used = int((lengths > 0).sum())
        fixed = max(1, used // 4)
        moved = fixed + (places - fixed + turn * (used - fixed)) % max(1, amount - fixed)
        return jnp.zeros((amount,), jnp.int32).at[ranking[jnp.where(places < fixed, places, moved)]].set(jnp.asarray(lengths, jnp.int32))

    lengths = jnp.where(number % 4 == 0, named(packed, number // 4), named(ordinary, number - number // 4 - 1))
    mixed = jax.random.permutation(jax.random.fold_in(own, 3), amount)
    donor, receiver = mixed[0:amount // 2 * 2:2], mixed[1:amount // 2 * 2:2]
    margin = jnp.minimum(lengths[donor] - 1, bound - lengths[receiver]) // 2
    margin = jnp.where((donor == ranking[0]) | (receiver == ranking[0]) | (lengths[receiver] == 0), 0, jnp.maximum(margin, 0))
    moved = jax.random.randint(jax.random.fold_in(own, 4), (amount // 2,), 0, 1 << 20) % (margin + 1)
    lengths = lengths.at[donor].add(-moved).at[receiver].add(moved)
    members = jnp.searchsorted(jnp.cumsum(lengths), jnp.arange(rows * top), side="right").astype(jnp.int32)
    table = members.reshape(top, rows).T
    table = table[jax.random.permutation(jax.random.fold_in(own, 1), rows)]
    turn = jax.random.randint(jax.random.fold_in(own, 2), (rows, 1), 0, top)
    return jnp.take_along_axis(table, (jnp.arange(top)[None, :] + turn) % top, axis=1)


def shares(count, total, reach, lean, full):
    portions = [(1 << 20) // math.isqrt(standing ** lean) + 1 for standing in range(1, count + 1)]
    largest = reach if full else min(reach, max(-(-total // count), total * portions[0] // sum(portions)))
    least = 1 if total - largest >= count - 1 else 0
    counts, surplus = [largest] + [least] * (count - 1), total - largest - least * (count - 1)
    while surplus > 0:
        free = [i for i in range(1, count) if counts[i] < largest] or [i for i in range(1, count) if counts[i] < reach]
        whole, remaining = sum([portions[i] for i in free]), surplus
        for i in free:
            more = min(reach - counts[i], max(1, remaining * portions[i] // whole), surplus)
            counts[i] = counts[i] + more
            surplus = surplus - more
    return np.array(counts)


def centred(own_key, extent, scale, most, split=(), held_as=jnp.bfloat16):
    values = jax.random.normal(own_key, extent, jnp.float32) * scale
    if len(split) > 0:
        values = steps_of(own_key, extent, split, -0.22, 0.18) * values
    return jnp.clip(values, min=-most, max=most).astype(held_as)


def setup_inputs(seed: int = 0, part: int = 0) -> dict:
    key_list = jax.random.split(jax.random.key(seed), 10)
    own_keys = jax.random.split(jax.random.fold_in(key_list[9], part), 10)
    tokens_q = centred(own_keys[0], (TOKENS, D), 120.0, 448.0, ((0, 16),))
    token_scale = jnp.clip(jnp.exp(math.log(0.03) - 2.3025851 * jax.random.uniform(own_keys[1], (TOKENS, D // QB), jnp.float32) ** steps_of(own_keys[1], (TOKENS, D // QB), ((0, 16),), -0.2, 0.2)), 0.003, 0.03)
    residual = centred(own_keys[2], (TOKENS, D), 1.0, 6.0, ((0, 16),))
    expert_ids_keys = jax.random.split(jax.random.fold_in(own_keys[3], 1), TOKENS // TOK_DEV)
    expert_ids_turns = jax.random.permutation(jax.random.fold_in(own_keys[3], 3), TOKENS // TOK_DEV)
    expert_ids = jax.vmap(lambda own, number: deal_out(jax.random.fold_in(own_keys[3], 2), own, number, TOK_DEV, EXPERTS, TOP, CAP, 2))(expert_ids_keys, expert_ids_turns).reshape((TOKENS, TOP))
    gate_values = jnp.clip(0.1 + 0.9 * jax.random.uniform(own_keys[4], (TOKENS, TOP), jnp.float32) ** steps_of(own_keys[4], (TOKENS, TOP), ((0, 16),), -0.2, 0.2), 0.1, 1.0)
    w_gate = centred(key_list[5], (EXPERTS, D, FF), D ** -0.5, 0.09375, ((0, 16),))
    w_up = centred(key_list[6], (EXPERTS, D, FF), D ** -0.5, 0.09375, ((0, 16),))
    w_down = centred(key_list[7], (EXPERTS, FF, D), FF ** -0.5, 0.1875, ((0, 16),))
    norm_gain = jnp.clip(1.0 + 0.1 * jax.random.normal(key_list[8], (D,), jnp.float32), 0.5, 1.5)
    return dict(tokens_q=tokens_q, token_scale=token_scale, residual=residual, expert_ids=expert_ids, gate_values=gate_values, w_gate=w_gate, w_up=w_up, w_down=w_down, norm_gain=norm_gain)


def slot_of(flat_ids):
    hot = (flat_ids[:, None] == jnp.arange(EXPERTS, dtype=jnp.int32)[None, :]).astype(jnp.int32)
    before = jnp.cumsum(hot, axis=0) - hot
    return lax.optimization_barrier(jnp.sum(before * hot, axis=1)).astype(jnp.int32)

def dequant(payload, scales):
    count = payload.shape[0]
    blocks = payload.astype(jnp.float32).reshape(count, D // QB, QB) * scales[:, :, None]
    return blocks.reshape(count, D).astype(jnp.bfloat16)

def expert_rows(inputs, gates, gate_matrix, up_matrix, down_matrix):
    gate_part = jnp.dot(inputs, gate_matrix, preferred_element_type=jnp.float32)
    up_part = jnp.dot(inputs, up_matrix, preferred_element_type=jnp.float32)
    hidden = (jax.nn.silu(gate_part) * up_part).astype(jnp.bfloat16)
    output = jnp.dot(hidden, down_matrix, preferred_element_type=jnp.float32)
    return (output * gates[:, None]).astype(jnp.bfloat16)

def reference(tokens_q, token_scale, residual, expert_ids, gate_values, w_gate, w_up, w_down, norm_gain):
    inputs = dequant(tokens_q, token_scale)
    per_source = expert_ids.reshape(N_EP, TOK_DEV * TOP)
    slots = jax.vmap(slot_of)(per_source)
    source = jnp.arange(N_EP, dtype=jnp.int32)[:, None] * jnp.ones((1, TOK_DEV * TOP), jnp.int32)
    owner = source * TOK_DEV + (jnp.arange(TOK_DEV * TOP, dtype=jnp.int32) // TOP)[None, :]
    where_slot = source * CAP + slots
    table_token = jnp.zeros((EXPERTS, N_EP * CAP), jnp.int32).at[per_source, where_slot].set(owner)
    table_gate = jnp.zeros((EXPERTS, N_EP * CAP), jnp.float32).at[per_source, where_slot].set(gate_values.reshape(N_EP, TOK_DEV * TOP))

    def one_expert(total, expert):
        rows_index = table_token[expert]
        output = expert_rows(inputs[rows_index], table_gate[expert], w_gate[expert], w_up[expert], w_down[expert])
        return (total.at[rows_index].add(output.astype(jnp.float32)), None)
    total, unused = lax.scan(one_expert, jnp.zeros((TOKENS, D), jnp.float32), jnp.arange(EXPERTS, dtype=jnp.int32))
    mixed = total + residual.astype(jnp.float32)
    new_residual = mixed.astype(jnp.bfloat16)
    meansq = lax.optimization_barrier(jnp.mean(mixed * mixed, axis=-1, keepdims=True))
    normed = mixed * lax.rsqrt(meansq + 1e-06) * norm_gain
    blocks = normed.reshape(TOKENS, D // QB, QB)
    next_scale = (lax.optimization_barrier(jnp.max(jnp.abs(blocks), axis=-1)) + 1e-06) / 448.0
    next_q = (blocks / next_scale[:, :, None]).reshape(TOKENS, D).astype(jnp.bfloat16)
    return (new_residual, next_q, next_scale)
```

```python
import functools

import jax
import jax.numpy as jnp
from jax import lax
from jax.experimental import pallas as pl
from jax.experimental.pallas import tpu as pltpu
from jax.sharding import PartitionSpec as P

LANES = 128


def prep_kernel(experts, q_ref, scale_ref, ids_ref, gates_ref, out_ref):
    rows, width = q_ref.shape
    blocks = scale_ref.shape[0]
    step = width // blocks
    scale = scale_ref[...].T
    for b in range(blocks):
        cols = slice(b * step, (b + 1) * step)
        out_ref[:, cols] = (q_ref[:, cols].astype(jnp.float32) * scale[:, b : b + 1]).astype(
            jnp.bfloat16
        )
    ids = ids_ref[...].T
    gates = gates_ref[...].T
    lane = lax.broadcasted_iota(jnp.int32, (rows, LANES), 1)
    slot = jnp.where(
        lane >= 2 * experts, lane - 2 * experts, jnp.where(lane >= experts, lane - experts, lane)
    )
    dense = jnp.zeros((rows, LANES), jnp.float32)
    for k in range(ids.shape[1]):
        dense = dense + jnp.where(slot == ids[:, k : k + 1], gates[:, k : k + 1], 0.0)
    high = dense.astype(jnp.bfloat16).astype(jnp.float32)
    middle = (dense - high).astype(jnp.bfloat16).astype(jnp.float32)
    low = dense - high - middle
    parts = jnp.where(
        lane < experts,
        high,
        jnp.where(lane < 2 * experts, middle, jnp.where(lane < 3 * experts, low, 0.0)),
    )
    out_ref[:, width:] = parts.astype(jnp.bfloat16)


def prepare(tokens_q, token_scale, expert_ids, gate_values, experts):
    rows, width = tokens_q.shape
    return pl.pallas_call(
        functools.partial(prep_kernel, experts),
        out_shape=jax.ShapeDtypeStruct((rows, width + LANES), jnp.bfloat16),
        name="prepare",
    )(tokens_q, token_scale.T, expert_ids.T, gate_values.T)


def expert_kernel(
    steps_in, experts, me_ref, x0, x1, x2, x3, gate_w, up_w, down_w, own0, own1, other, x_s, h_s, g_s
):
    i = pl.program_id(0)
    rows, extended = x0.shape
    width = extended - LANES

    @pl.when(i == 0)
    def _():
        me = me_ref[0]
        lane = lax.broadcasted_iota(jnp.int32, (rows, LANES), 1)
        mine = (lane == me) | (lane == me + experts) | (lane == me + 2 * experts)
        for n, x in enumerate((x0, x1, x2, x3)):
            x_s[n * rows : (n + 1) * rows, :] = x[:, :width]
            parts = jnp.where(mine, x[:, width:].astype(jnp.float32), 0.0)
            g_s[n * rows : (n + 1) * rows, :] = jnp.sum(parts, axis=1, keepdims=True)

    @pl.when(i < steps_in)
    def _():
        x = x_s[...]
        gate = jnp.dot(x, gate_w[0], preferred_element_type=jnp.float32)
        up = jnp.dot(x, up_w[0], preferred_element_type=jnp.float32)
        h_s[i] = (gate * jax.nn.sigmoid(gate) * up).astype(jnp.bfloat16)

    @pl.when(i >= steps_in)
    def _():
        block = h_s.shape[2]
        total = jnp.dot(h_s[0], down_w[0, :block], preferred_element_type=jnp.float32)
        for k in range(1, steps_in):
            total = total + jnp.dot(
                h_s[k], down_w[0, k * block : (k + 1) * block], preferred_element_type=jnp.float32
            )
        part = (total * g_s[...]).astype(jnp.bfloat16)
        own0[...] = part[:rows]
        own1[...] = part[rows : 2 * rows]
        other[...] = part[2 * rows :]


def expert(me, xs, w_gate, w_up, w_down):
    experts = lax.axis_size("ep")
    rows, extended = xs[0].shape
    width = extended - LANES
    hidden = w_gate.shape[2]
    steps_in, steps_out = 4, 4
    block_in, block_out = hidden // steps_in, width // steps_out
    x_spec = pl.BlockSpec((rows, extended), lambda i: (0, 0))
    in_spec = pl.BlockSpec((1, width, block_in), lambda i: (0, 0, jnp.minimum(i, steps_in - 1)))
    after = lambda i: jnp.maximum(i - steps_in, 0)
    out = lambda r: pl.BlockSpec((r, block_out), lambda i: (0, after(i)))
    return pl.pallas_call(
        functools.partial(expert_kernel, steps_in, experts),
        grid=(steps_in + steps_out,),
        in_specs=[pl.BlockSpec(memory_space=pltpu.SMEM)]
        + [x_spec] * 4
        + [in_spec] * 2
        + [pl.BlockSpec((1, hidden, block_out), lambda i: (0, 0, after(i)))],
        out_specs=[out(rows), out(rows), out(2 * rows)],
        out_shape=[
            jax.ShapeDtypeStruct((rows, width), jnp.bfloat16),
            jax.ShapeDtypeStruct((rows, width), jnp.bfloat16),
            jax.ShapeDtypeStruct((2 * rows, width), jnp.bfloat16),
        ],
        scratch_shapes=[
            pltpu.VMEM((4 * rows, width), jnp.bfloat16),
            pltpu.VMEM((steps_in, 4 * rows, block_in), jnp.bfloat16),
            pltpu.VMEM((4 * rows, 1), jnp.float32),
        ],
        compiler_params=pltpu.CompilerParams(dimension_semantics=("arbitrary",)),
        cost_estimate=pl.CostEstimate(
            flops=2 * 4 * rows * width * hidden * 3,
            transcendentals=4 * rows * hidden,
            bytes_accessed=3 * width * hidden * 2 + 16 * rows * width,
        ),
        name="expert",
    )(me, *xs, w_gate, w_up, w_down)


def add_kernel(*refs):
    *ins, out = refs
    total = ins[0][...].astype(jnp.float32)
    for ref in ins[1:]:
        total = total + ref[...].astype(jnp.float32)
    out[...] = total.astype(jnp.bfloat16)


def add(name, own, pair, half, *more):
    rows, width = own.shape
    whole = pl.BlockSpec((rows, width), lambda i: (0, 0))
    return pl.pallas_call(
        add_kernel,
        grid=(1,),
        in_specs=[whole, pl.BlockSpec((rows, width), lambda i: (half, 0))] + [whole] * len(more),
        out_specs=whole,
        out_shape=jax.ShapeDtypeStruct((rows, width), jnp.bfloat16),
        name=name,
    )(own, pair, *more)


def final_kernel(*refs):
    *sums, residual, gain, new_residual, next_q, next_scale = refs
    rows, width = residual.shape
    blocks = next_scale.shape[0]
    step = width // blocks
    square = jnp.zeros((rows, step), jnp.float32)
    mixed = []
    for b in range(blocks):
        cols = slice(b * step, (b + 1) * step)
        value = sums[0][:, cols].astype(jnp.float32)
        for ref in sums[1:]:
            value = value + ref[:, cols].astype(jnp.float32)
        value = value + residual[:, cols].astype(jnp.float32)
        new_residual[:, cols] = value.astype(jnp.bfloat16)
        square = square + value * value
        mixed.append(value)
    inverse = lax.rsqrt(jnp.sum(square, axis=1, keepdims=True) / width + 1e-06)
    scales = []
    for b in range(blocks):
        cols = slice(b * step, (b + 1) * step)
        normed = mixed[b] * inverse * gain[:, cols]
        scale = (jnp.max(jnp.abs(normed), axis=1, keepdims=True) + 1e-06) / 448.0
        next_q[:, cols] = (normed / scale).astype(jnp.bfloat16)
        scales.append(scale)
    next_scale[...] = jnp.concatenate(scales, axis=1).T


def finish(own, pair, sums, residual, gain, blocks):
    rows, width = residual.shape
    whole = pl.BlockSpec((rows, width), lambda i: (0, 0))
    new_residual, next_q, next_scale = pl.pallas_call(
        final_kernel,
        grid=(1,),
        in_specs=[whole, whole] + [whole] * len(sums) + [whole, pl.BlockSpec((1, width), lambda i: (0, 0))],
        out_specs=[whole, whole, pl.BlockSpec((blocks, rows), lambda i: (0, 0))],
        out_shape=[
            jax.ShapeDtypeStruct((rows, width), jnp.bfloat16),
            jax.ShapeDtypeStruct((rows, width), jnp.bfloat16),
            jax.ShapeDtypeStruct((blocks, rows), jnp.float32),
        ],
        name="finish",
    )(own, pair, *sums, residual, gain.reshape(1, width))
    return new_residual, next_q, next_scale.T


def per_device(
    tokens_q, token_scale, residual, expert_ids, gate_values, w_gate, w_up, w_down, norm_gain
):
    devices = lax.axis_size("ep")
    layers = devices // 4
    swap_c = [(d, d ^ 1) for d in range(devices)]
    swap_y = [(d, d ^ 2) for d in range(devices)]
    shift = lambda s: [(d, (d + 4 * s) % devices) for d in range(devices)]
    send = lambda a, perm: lax.ppermute(a, "ep", perm)
    me = lax.axis_index("ep").astype(jnp.int32).reshape(1)
    own = prepare(tokens_q, token_scale, expert_ids, gate_values, devices)
    arrived = [own] + [send(own, shift(s)) for s in range(1, layers)]
    sums = []
    for s in range(layers):
        a = arrived[s]
        b = send(a, swap_y)
        xs = (a, b, send(a, swap_c), send(b, swap_c))
        own0, own1, other = expert(me, xs, w_gate, w_up, w_down)
        pair = send(other, swap_c)
        across = send(add("add_pair", own1, pair, 1), swap_y)
        if s == 0:
            first = (own0, pair, across)
        else:
            sums.append(send(add("add_row", own0, pair, 0, across), shift(layers - s)))
    return finish(first[0], first[1], [first[2]] + sums, residual, norm_gain, token_scale.shape[1])


def solution(mesh):
    rows = P(("dp", "ep"), None)
    weights = P("ep", None, None)
    return jax.shard_map(
        per_device,
        mesh=mesh,
        in_specs=(rows,) * 5 + (weights,) * 3 + (P(),),
        out_specs=(rows,) * 3,
        check_vma=False,
    )
```
